256 devices in a mesh: grp: 2 (over core), gx: 16 (over y, x), gy: 8 (over z).
Axes of the slice: x: 4, y: 4, z: 8, core: 2. Of those that a mesh axis runs over, the one named last changes fastest.
Arguments:
- fluxes: float32 [2, 10, 262144], P('grp', None, ('gx', 'gy')), may hold values from -6 to 6
- weights: bfloat16 [2, 64, 4096, 1024], P('grp', None, 'gx', 'gy'), may hold values from 0.049804688 to 1
- land_rows: int32 [2, 4096, 512], P('grp', 'gx', 'gy'), may hold values from 0 to 2047
- owners: int32 [2, 16, 8, 256, 1], P('grp', 'gx', 'gy'), may hold values from 0 to 127; in each aligned block of 256 rows (0 to 255, 256 to 511, ..., all dimensions but the last counted through in order) at most 4 rows name the same one
- elev_class: int32 [2, 4096, 1024], P('grp', 'gx', 'gy'), may hold values from 0 to 9
- ice_mask: int32 [2, 4096, 1024], P('grp', 'gx', 'gy'), may hold values 0 or 1
- bed: float32 [2, 4096, 1024], P('grp', 'gx', 'gy'), may hold values from -0.5 to 1
- thickness: float32 [2, 4096, 1024], P('grp', 'gx', 'gy'), may hold values from 0 to 2
- diffusivity: float32 [2, 4096, 1024], P('grp', 'gx', 'gy'), may hold values from 0.02 to 0.24
Outputs:
- land_fields: float32 [2, 2, 262144], P('grp', None, ('gx', 'gy'))
- thickness_new: float32 [2, 4096, 1024], P('grp', 'gx', 'gy')
The draws below stay inside these ranges and needn't reach their ends.
Inputs may be any that keep to these rules, and one draw needn't show every extreme that they name: `owners`: within each ice device's 256 rows no land owner is named by more than 4 rows, a bound that some block reaches.
All inputs are finite; a program needn't handle non-finite values. No bound on the sum of `ice_mask` on one device may be relied on, other than what follows from the above.
Results may differ from the reference program's by a relative error of at most 0.00051.
Values may be sent and summed in bfloat16 or wider, within the bound.
No kernel may reach another device: no remote copies, remote signals or barrier semaphores. Data moves between devices by JAX's collectives and lax.ppermute only.
A program may use at most 64 MiB of HBM per device.

```python
import math
import jax
import jax.numpy as jnp
import numpy as np
from jax import lax

EC = 10
BL = 64
STEPS = 4
LC = 2048
RX = 256
RY = 128
CAP = 4
NX = 4096
NY = 1024
LAND = 262144
N_GX = 16
N_GY = 8


def with_ends(values, own_key, smallest, high):
    shape = values.shape
    index_at = [jax.random.randint(jax.random.fold_in(own_key, axis), (), 0, shape[axis]) for axis in range(len(shape))]
    values = values.at[tuple(index_at)].set(smallest)
    longest = shape.index(max(shape))
    index_at[longest] = (index_at[longest] + 1) % shape[longest]
    return values.at[tuple(index_at)].set(high)


def levels(rng, shape, split, least, top_value):
    def one(axis_at, shards_of):
        steps = jax.random.uniform(jax.random.fold_in(jax.random.fold_in(rng, 6), axis_at), (shards_of,), jnp.float32, least / len(split), top_value / len(split))
        return jnp.repeat(jnp.exp(steps), shape[axis_at] // shards_of).reshape((-1,) + (1,) * (len(shape) - axis_at - 1))

    factor_of = one(*split[0])
    for cut in split[1:]:
        factor_of = factor_of * one(*cut)
    return factor_of


def shared_out(rng, own, number, rows, number_of, top, limit, slope):
    sequence = jax.random.permutation(rng, number_of)
    crowded, usual = shares(number_of, rows * top, limit, slope, True), shares(number_of, rows * top, limit, slope, False)
    places = jnp.arange(number_of)

    def named(tallies, offset_by):
        used = int((tallies > 0).sum())
        fixed = max(1, used // 4)
        moved = fixed + (places - fixed + offset_by * (used - fixed)) % max(1, number_of - fixed)
        return jnp.zeros((number_of,), jnp.int32).at[sequence[jnp.where(places < fixed, places, moved)]].set(jnp.asarray(tallies, jnp.int32))

    tallies = jnp.where(number % 4 == 0, named(crowded, number // 4), named(usual, number - number // 4 - 1))
    mixed = jax.random.permutation(jax.random.fold_in(own, 3), number_of)
    source_of, receiver = mixed[0:number_of // 2 * 2:2], mixed[1:number_of // 2 * 2:2]
    room = jnp.minimum(tallies[source_of] - 1, limit - tallies[receiver]) // 2
    room = jnp.where((source_of == sequence[0]) | (receiver == sequence[0]) | (tallies[receiver] == 0), 0, jnp.maximum(room, 0))
    moved = jax.random.randint(jax.random.fold_in(own, 4), (number_of // 2,), 0, 1 << 20) % (room + 1)
    tallies = tallies.at[source_of].add(-moved).at[receiver].add(moved)
    labels = jnp.searchsorted(jnp.cumsum(tallies), jnp.arange(rows * top), side="right").astype(jnp.int32)
    listing = labels.reshape(top, rows).T
    listing = listing[jax.random.permutation(jax.random.fold_in(own, 1), rows)]
    offset_by = jax.random.randint(jax.random.fold_in(own, 2), (rows, 1), 0, top)
    return jnp.take_along_axis(listing, (jnp.arange(top)[None, :] + offset_by) % top, axis=1)


def shares(number_of, total, reach, skew, full):
    loads = [(1 << 20) // math.isqrt(grade ** skew) + 1 for grade in range(1, number_of + 1)]
    largest = reach if full else min(reach, max(-(-total // number_of), total * loads[0] // sum(loads)))
    least = 1 if total - largest >= number_of - 1 else 0
    counts, surplus = [largest] + [least] * (number_of - 1), total - largest - least * (number_of - 1)
    while surplus > 0:
        candidates = [i for i in range(1, number_of) if counts[i] < largest] or [i for i in range(1, number_of) if counts[i] < reach]
        mass, budget = sum([loads[i] for i in candidates]), surplus
        for i in candidates:
            extra = min(reach - counts[i], max(1, budget * loads[i] // mass), surplus)
            counts[i] = counts[i] + extra
            surplus = surplus - extra
    return np.array(counts)


def normal_values(own_key, extent, scale, most, cuts=(), held_as=jnp.bfloat16):
    array = scale * jax.random.normal(own_key, extent, jnp.float32)
    if cuts:
        array = array * levels(own_key, extent, cuts, -0.22, 0.18)
    return jnp.clip(array, -most, most).astype(held_as)


def setup_inputs(seed: int = 0) -> dict:
    keys = jax.random.split(jax.random.key(seed), 10)
    fluxes = normal_values(keys[0], (2, EC, LAND), 1.0, 6.0, ((0, 2), (2, 128)), jnp.float32)
    weights = jnp.clip(jnp.exp(math.log(1.0) - 2.9996462 * jax.random.uniform(keys[1], (2, BL, NX, NY), jnp.float32) ** levels(keys[1], (2, BL, NX, NY), ((0, 2), (2, 16), (3, 8)), -0.2, 0.2)), 0.049804688, 1.0).astype(jnp.bfloat16)
    land_rows = with_ends(jax.random.randint(keys[2], (2, NX, N_GY * BL), 0, LC), jax.random.fold_in(keys[2], 1), 0, LC - 1).astype(jnp.int32)
    owners_keys = jax.random.split(jax.random.fold_in(keys[3], 1), 2 * N_GX * N_GY * RX // RX)
    owners_turns = jax.random.permutation(jax.random.fold_in(keys[3], 3), 2 * N_GX * N_GY * RX // RX)
    owners = jax.vmap(lambda own, number: shared_out(jax.random.fold_in(keys[3], 2), own, number, RX, N_GX * N_GY, 1, CAP, 2))(owners_keys, owners_turns).reshape((2, N_GX, N_GY, RX, 1))
    elev_class = with_ends(jax.random.randint(keys[4], (2, NX, NY), 0, EC), jax.random.fold_in(keys[4], 1), 0, EC - 1).astype(jnp.int32)
    ice_mask = with_ends((jax.random.randint(keys[5], (2, NX, NY), 0, 4) < 3).astype(jnp.int32), jax.random.fold_in(keys[5], 1), 0, 1)
    bed = jnp.clip(-0.5 + 1.5 * jax.random.uniform(keys[6], (2, NX, NY), jnp.float32) ** levels(keys[6], (2, NX, NY), ((0, 2), (1, 16), (2, 8)), -0.2, 0.2), -0.5, 1.0)
    thickness = jnp.clip(2.0 * jax.random.uniform(keys[7], (2, NX, NY), jnp.float32) ** levels(keys[7], (2, NX, NY), ((0, 2), (1, 16), (2, 8)), -0.2, 0.2), 0.0, 2.0)
    diffusivity = jnp.clip(0.02 + 0.22 * jax.random.uniform(keys[8], (2, NX, NY), jnp.float32) ** levels(keys[8], (2, NX, NY), ((0, 2), (1, 16), (2, 8)), -0.2, 0.2), 0.02, 0.24)
    return dict(fluxes=fluxes, weights=weights, land_rows=land_rows, owners=owners, elev_class=elev_class, ice_mask=ice_mask, bed=bed, thickness=thickness, diffusivity=diffusivity)


FULL_PRECISION = lax.Precision.HIGHEST
SMB_RATE = 0.5


def round_half(values):
    return lax.optimization_barrier(values.astype(jnp.bfloat16)).astype(jnp.float32)


def relax_step(thick_pad, bed_pad, diff_pad, source, inside):
    surface = bed_pad + thick_pad
    centre_surface = surface[1:-1, 1:-1]
    centre_diff = diff_pad[1:-1, 1:-1]
    change = jnp.zeros_like(centre_surface)
    neighbours = ((surface[2:, 1:-1], diff_pad[2:, 1:-1]), (surface[:-2, 1:-1], diff_pad[:-2, 1:-1]),
                  (surface[1:-1, 2:], diff_pad[1:-1, 2:]), (surface[1:-1, :-2], diff_pad[1:-1, :-2]))
    for near_surface, near_diff in neighbours:
        change = change + 0.5 * (centre_diff + near_diff) * (near_surface - centre_surface)
    return jnp.maximum(thick_pad[1:-1, 1:-1] + change + SMB_RATE * source, 0.0) * inside


def reference(fluxes, weights, land_rows, owners, elev_class, ice_mask, bed, thickness, diffusivity):
    groups = N_GX * N_GY
    land_flux = fluxes[0]
    owner_grid = jnp.transpose(owners[1, :, :, :, 0], (0, 2, 1))
    local_rows = land_rows[1].reshape(N_GX, RX, N_GY, BL)
    target = owner_grid[..., None] * LC + local_rows
    blocks = jnp.transpose(weights[1].reshape(BL, N_GX, RX, N_GY, RY), (1, 0, 2, 3, 4))
    keep_mask = ice_mask[1].astype(jnp.float32)
    chosen = elev_class[1].reshape(N_GX, RX, N_GY, RY)

    def remap_rows(inputs):
        weight_block, target_rows, class_pick, mask_block = inputs
        weight32 = weight_block.astype(jnp.float32)
        weight_total = jnp.sum(weight32, axis=0)
        gathered = round_half(land_flux[:, target_rows])
        remapped = jnp.einsum("ergb,brgj->ergj", gathered, weight32, precision=FULL_PRECISION) / weight_total
        return mask_block * jnp.take_along_axis(remapped, class_pick[None], axis=0)[0]

    source = lax.map(remap_rows, (blocks, target, chosen, keep_mask.reshape(N_GX, RX, N_GY, RY)))
    source = source.reshape(NX, NY)
    bed_local = bed[1]
    bed_pad = jnp.pad(bed_local, 1)
    diff_pad = jnp.pad(diffusivity[1], 1)
    thick_now = thickness[1]
    for sweep in range(STEPS):
        thick_now = relax_step(jnp.pad(thick_now, 1), bed_pad, diff_pad, source, 1.0)
    surface = bed_local + thick_now
    ice_fraction = keep_mask * jnp.minimum(thick_now, 1.0)
    fields = jnp.stack([surface, ice_fraction, jnp.ones_like(surface)]).reshape(3, N_GX, RX, N_GY, RY)

    def return_rows(inputs):
        weight_block, field_block = inputs
        weight32 = weight_block.astype(jnp.float32)
        weight_total = jnp.sum(weight32, axis=0)
        scaled = round_half(field_block / weight_total)
        return jnp.einsum("brgj,qrgj->qrgb", weight32, scaled, precision=FULL_PRECISION)

    partial_value = lax.map(return_rows, (blocks, jnp.transpose(fields, (1, 0, 2, 3, 4))))
    partial_value = jnp.transpose(partial_value, (1, 0, 2, 3, 4)).reshape(3, -1)
    land_sums = jax.ops.segment_sum(partial_value.T, target.reshape(-1), num_segments=groups * LC).T
    averaged = land_sums[:2] / jnp.maximum(land_sums[2], 1.0)
    land_fields = jnp.stack([averaged, jnp.zeros_like(averaged)])
    thickness_new = jnp.stack([jnp.zeros_like(thick_now), thick_now])
    return land_fields, thickness_new
```

```python
import jax
import jax.numpy as jnp
from jax import lax
from jax.experimental import pallas as pl
from jax.experimental.pallas import tpu as pltpu
from jax.sharding import PartitionSpec as P

STEPS = 4
SMB_RATE = 0.5
LOW = 256
PLANES = ("gx", "gy")
F32 = jnp.float32
BF16 = jnp.bfloat16


def neighbours(axis, value, low_edge, high_edge):
    count = lax.axis_size(axis)
    forward = [(i, i + 1) for i in range(count - 1)]
    backward = [(i + 1, i) for i in range(count - 1)]
    from_low = lax.ppermute(high_edge, axis, forward)
    from_high = lax.ppermute(low_edge, axis, backward)
    return from_low, from_high


def padded_halo(block, width):
    count, rows, cols = block.shape
    turn = lambda part: jnp.transpose(part, (0, 2, 1))
    left, right = neighbours(
        "gy", block, turn(block[:, :, :width]), turn(block[:, :, cols - width :])
    )
    block = jnp.concatenate([turn(left), block, turn(right)], axis=2)
    above, below = neighbours("gx", block, block[:, :width], block[:, rows - width :])
    return jnp.concatenate([above, block, below], axis=1)


def pick_kernel(table_ref, index_ref, out_ref):
    sources = index_ref.shape[0]
    classes = out_ref.shape[1]
    high_count = table_ref.shape[0] // 16
    table = table_ref[...]
    low_iota = lax.broadcasted_iota(jnp.int32, (LOW, 128), 0)
    for s in range(0, sources, 2):
        hot = []
        high = []
        for d in range(2):
            row = index_ref[s + d : s + d + 1, :]
            hot.append((low_iota == (row & (LOW - 1))).astype(F32).astype(BF16))
            high.append(jnp.broadcast_to(row // LOW, (16, 128)))
        found = jnp.dot(
            table, jnp.concatenate(hot, axis=1), preferred_element_type=F32
        )
        for d in range(2):
            part = found[:, 128 * d : 128 * d + 128]
            total = part[:16]
            for h in range(1, high_count):
                total = jnp.where(high[d] == h, part[16 * h : 16 * h + 16], total)
            out_ref[s + d] = total[:classes].astype(BF16)


def pick(table, asked, classes):
    sources = asked.shape[0]
    step = 16
    return pl.pallas_call(
        pick_kernel,
        grid=(sources // step,),
        in_specs=[
            pl.BlockSpec(table.shape, lambda i: (0, 0)),
            pl.BlockSpec((step, 128), lambda i: (i, 0)),
        ],
        out_specs=pl.BlockSpec((step, classes, 128), lambda i: (i, 0, 0)),
        out_shape=jax.ShapeDtypeStruct((sources, classes, 128), BF16),
        name="pick",
    )(table, asked)


def scatter_kernel(index_ref, value_ref, out_ref):
    sources = index_ref.shape[0]
    high_count = out_ref.shape[0] // 3
    low_iota = lax.broadcasted_iota(jnp.int32, (LOW, 128), 0)
    high_iota = lax.broadcasted_iota(jnp.int32, (high_count, 128), 0)
    hot = []
    spread = []
    for s in range(sources):
        row = index_ref[s : s + 1, :]
        hot.append((low_iota == (row & (LOW - 1))).astype(F32).astype(BF16))
        mine = high_iota == row // LOW
        values = value_ref[s]
        first = values.astype(BF16).astype(F32)
        rest = values - first
        rows = []
        for part in (first, rest):
            for q in range(3):
                rows.append(jnp.where(mine, part[q : q + 1], 0.0))
        spread.append(jnp.concatenate(rows, axis=0).astype(BF16))
    sums = lax.dot_general(
        jnp.concatenate(spread, axis=1),
        jnp.concatenate(hot, axis=1),
        (((1,), (1,)), ((), ())),
        preferred_element_type=F32,
    )
    sums = sums[: 3 * high_count] + sums[3 * high_count :]

    @pl.when(pl.program_id(0) == 0)
    def _():
        out_ref[...] = sums

    @pl.when(pl.program_id(0) > 0)
    def _():
        out_ref[...] += sums


def scatter(asked, values, high_count):
    sources = asked.shape[0]
    step = 16
    return pl.pallas_call(
        scatter_kernel,
        grid=(sources // step,),
        in_specs=[
            pl.BlockSpec((step, 128), lambda i: (i, 0)),
            pl.BlockSpec((step, 3, 128), lambda i: (i, 0, 0)),
        ],
        out_specs=pl.BlockSpec((3 * high_count, LOW), lambda i: (0, 0)),
        out_shape=jax.ShapeDtypeStruct((3 * high_count, LOW), F32),
        name="scatter",
    )(asked, values)


def relax(thick, bed, diff, source, inside):
    surface = bed + thick
    centre = surface[1:-1, 1:-1]
    centre_diff = diff[1:-1, 1:-1]
    change = jnp.zeros_like(centre)
    for near, near_diff in (
        (surface[2:, 1:-1], diff[2:, 1:-1]),
        (surface[:-2, 1:-1], diff[:-2, 1:-1]),
        (surface[1:-1, 2:], diff[1:-1, 2:]),
        (surface[1:-1, :-2], diff[1:-1, :-2]),
    ):
        change = change + 0.5 * (centre_diff + near_diff) * (near - centre)
    return jnp.maximum(thick[1:-1, 1:-1] + change + SMB_RATE * source, 0.0) * inside


def per_device(
    fluxes, weights, land_rows, owners, elev_class, ice_mask, bed, thickness, diffusivity
):
    groups = lax.axis_size("gx") * lax.axis_size("gy")
    is_ice = lax.axis_index("grp") == 1
    block_weights = weights[0]
    local_rows = land_rows[0]
    row_count, width = local_rows.shape
    col_count = block_weights.shape[2]
    classes, cells = fluxes.shape[1:]
    high_count = cells // LOW

    table = jnp.pad(fluxes[0].astype(BF16), ((0, 16 - classes), (0, 0)))
    table = jnp.transpose(table.reshape(16, high_count, LOW), (1, 0, 2)).reshape(-1, LOW)
    table = jnp.where(is_ice, lax.ppermute(table, "grp", [(0, 1)]), table)

    owner_row = owners.reshape(1, row_count)
    named = lax.broadcasted_iota(jnp.int32, (groups, row_count), 0) == owner_row
    earlier = lax.broadcasted_iota(jnp.int32, (row_count, row_count), 0) < (
        lax.broadcasted_iota(jnp.int32, (row_count, row_count), 1)
    )
    rank = jnp.dot(named.astype(BF16), earlier.astype(BF16), preferred_element_type=F32)
    place = jnp.stack([named & (rank == k) for k in range(4)]).astype(BF16)
    digits = jnp.concatenate([local_rows // 8, local_rows % 8], axis=1).astype(BF16)
    wanted = jnp.einsum("kor,rb->kob", place, digits, preferred_element_type=F32)
    wanted = (8.0 * wanted[..., :width] + wanted[..., width:]).astype(jnp.int32)
    wanted = [jnp.concatenate([wanted[k], wanted[k + 1]], axis=1) for k in (0, 2)]
    request = jnp.where(is_ice, wanted[0], lax.ppermute(wanted[1], "grp", [(1, 0)]))
    asked = lax.all_to_all(request, PLANES, split_axis=0, concat_axis=0, tiled=True)

    answer = pick(table, asked, classes)
    answer = answer.reshape(groups, classes // 2, 2, 128)
    answer = lax.all_to_all(answer, PLANES, split_axis=0, concat_axis=0, tiled=True)
    answer = answer.reshape(groups, classes, 2, width)
    other = lax.ppermute(answer, "grp", [(0, 1)])
    picked = sum(
        jnp.einsum(
            "or,oeb->reb",
            place[k],
            (answer, other)[k // 2][:, :, k % 2],
            preferred_element_type=F32,
        )
        for k in range(4)
    ).astype(BF16)

    weight_total = jnp.sum(block_weights, axis=0, dtype=F32)
    remapped = jnp.einsum(
        "reb,brj->erj", picked, block_weights, preferred_element_type=F32
    )
    keep_mask = ice_mask[0].astype(F32)
    level = jnp.arange(classes, dtype=jnp.int32)[:, None, None]
    source = keep_mask * (
        jnp.sum(jnp.where(elev_class[0][None] == level, remapped, 0.0), axis=0) / weight_total
    )

    fixed = padded_halo(jnp.stack([bed[0], diffusivity[0], thickness[0]]), STEPS)
    source_pad = padded_halo(source[None], STEPS - 1)[0]
    row_at = lax.axis_index("gx") * row_count - STEPS + lax.broadcasted_iota(
        jnp.int32, fixed.shape[1:], 0
    )
    col_at = lax.axis_index("gy") * col_count - STEPS + lax.broadcasted_iota(
        jnp.int32, fixed.shape[1:], 1
    )
    inside = (
        (row_at >= 0)
        & (row_at < row_count * lax.axis_size("gx"))
        & (col_at >= 0)
        & (col_at < col_count * lax.axis_size("gy"))
    ).astype(F32)
    bed_pad, diff_pad, thick = fixed[0], fixed[1], fixed[2]
    for step in range(STEPS):
        trim = lambda a, n: a[n : a.shape[0] - n, n : a.shape[1] - n] if n else a
        thick = relax(
            thick,
            trim(bed_pad, step),
            trim(diff_pad, step),
            trim(source_pad, step),
            trim(inside, step + 1),
        )

    surface = bed[0] + thick
    fraction = keep_mask * jnp.minimum(thick, 1.0)
    fields = (jnp.stack([surface, fraction, jnp.ones_like(surface)]) / weight_total).astype(BF16)
    partial = jnp.einsum("brj,qrj->qrb", block_weights, fields, preferred_element_type=F32)
    outgoing = jnp.einsum(
        "kor,qrb->koqb",
        place.astype(F32),
        partial,
        precision=lax.Precision.HIGHEST,
        preferred_element_type=F32,
    )
    outgoing = [jnp.concatenate([outgoing[k], outgoing[k + 1]], axis=2) for k in (0, 2)]
    sent = jnp.where(is_ice, outgoing[0], lax.ppermute(outgoing[1], "grp", [(1, 0)]))
    arrived = lax.all_to_all(sent, PLANES, split_axis=0, concat_axis=0, tiled=True)
    land_sums = scatter(asked, arrived, high_count)
    land_sums = land_sums + lax.ppermute(land_sums, "grp", [(1, 0)])
    land_sums = land_sums.reshape(3, cells)
    averaged = land_sums[:2] / jnp.maximum(land_sums[2], 1.0)
    land_fields = jnp.where(is_ice, 0.0, averaged)[None]
    thickness_new = jnp.where(is_ice, thick, 0.0)[None]
    return (land_fields, thickness_new)


def solution(mesh):
    return jax.shard_map(
        per_device,
        mesh=mesh,
        in_specs=(
            P("grp", None, ("gx", "gy")),
            P("grp", None, "gx", "gy"),
            P("grp", "gx", "gy"),
            P("grp", "gx", "gy", None, None),
            P("grp", "gx", "gy"),
            P("grp", "gx", "gy"),
            P("grp", "gx", "gy"),
            P("grp", "gx", "gy"),
            P("grp", "gx", "gy"),
        ),
        out_specs=(P("grp", None, ("gx", "gy")), P("grp", "gx", "gy")),
        check_vma=False,
    )
```

```python
import jax
import jax.numpy as jnp
from jax import lax
from jax.experimental import pallas as pl
from jax.experimental.pallas import tpu as pltpu
from jax.sharding import PartitionSpec as P

STEPS = 4
SMB_RATE = 0.5
LOW = 256
EDGE = 8
PLANES = ("gx", "gy")
F32 = jnp.float32
BF16 = jnp.bfloat16
EXACT = lax.Precision.HIGHEST
ROOM = pltpu.CompilerParams(vmem_limit_bytes=16 << 20)


def swap_cores(value):
    return lax.ppermute(value, "grp", [(0, 1), (1, 0)])


def ring(value, axis, step):
    count = lax.axis_size(axis)
    return lax.ppermute(value, axis, [(i, (i + step) % count) for i in range(count)])


def after(value, *others):
    return lax.optimization_barrier((value,) + others)[0]


def ones_where(mask):
    return jnp.where(mask, 1.0, 0.0).astype(BF16)


def head_kernel(owner_ref, rows_ref, low_ref, high_ref, place_ref):
    groups, row_count = low_ref.shape[0], owner_ref.shape[1]
    width = rows_ref.shape[0]
    named = lax.broadcasted_iota(jnp.int32, (groups, row_count), 0) == owner_ref[...]
    square = (row_count, row_count)
    earlier = lax.broadcasted_iota(jnp.int32, square, 0) < lax.broadcasted_iota(
        jnp.int32, square, 1
    )
    rank = jnp.dot(ones_where(named), ones_where(earlier), preferred_element_type=F32)
    rank = jnp.where(named, rank, -1.0)
    rows = rows_ref[...]
    digits = jnp.concatenate([rows >> 3, rows & 7], axis=0).astype(F32).astype(BF16)
    for half, out_ref in enumerate((low_ref, high_ref)):
        parts = []
        for k in (2 * half, 2 * half + 1):
            mine = ones_where(rank == k)
            place_ref[groups * k : groups * (k + 1), :] = mine
            found = lax.dot_general(
                mine, digits, (((1,), (1,)), ((), ())), preferred_element_type=F32
            )
            parts.append(8.0 * found[:, :width] + found[:, width:])
        out_ref[...] = jnp.concatenate(parts, axis=1).astype(jnp.int32)


def head(owner_row, rows, groups):
    row_count = owner_row.shape[1]
    lanes = 2 * rows.shape[0]
    return pl.pallas_call(
        head_kernel,
        out_shape=(
            jax.ShapeDtypeStruct((groups, lanes), jnp.int32),
            jax.ShapeDtypeStruct((groups, lanes), jnp.int32),
            jax.ShapeDtypeStruct((4 * groups, row_count), BF16),
        ),
        compiler_params=ROOM,
        name="head",
    )(owner_row, rows)


def hot_low(low, tiles):
    key = jnp.broadcast_to(low.astype(F32), (16, 128)).astype(BF16)
    one = jnp.ones((16, 128), BF16)
    zero = jnp.zeros((16, 128), BF16)
    return jnp.concatenate([jnp.where(tile == key, one, zero) for tile in tiles], axis=0)


def low_tiles():
    base = lax.broadcasted_iota(jnp.int32, (16, 128), 0)
    return [(base + 16 * i).astype(F32).astype(BF16) for i in range(LOW // 16)]


def pick_kernel(table_ref, index_ref, out_ref):
    sources = index_ref.shape[0]
    high_count = table_ref.shape[0] // 16
    table = table_ref[...]
    tiles = low_tiles()
    group = min(32, sources)

    def pick_group(i, carry):
        start = pl.multiple_of(i * group, group)
        block = index_ref[pl.ds(start, group), :]
        for s in range(0, group, 2):
            rows = [block[s + d : s + d + 1, :] for d in range(2)]
            hot = jnp.concatenate([hot_low(row & (LOW - 1), tiles) for row in rows], axis=1)
            found = jnp.dot(table, hot, preferred_element_type=F32)
            for d in range(2):
                high = jnp.broadcast_to(rows[d] // LOW, (16, 128))
                part = found[:, 128 * d : 128 * d + 128]
                total = part[:16]
                for h in range(1, high_count):
                    total = jnp.where(high == h, part[16 * h : 16 * h + 16], total)
                total = total.astype(BF16)
                for pair in range(out_ref.shape[1]):
                    out_ref[start + s + d, pair] = total[2 * pair : 2 * pair + 2]
        return carry

    lax.fori_loop(0, sources // group, pick_group, 0)


def pick(table, asked, classes):
    return pl.pallas_call(
        pick_kernel,
        out_shape=jax.ShapeDtypeStruct((asked.shape[0], classes // 2, 2, 128), BF16),
        compiler_params=ROOM,
        name="pick",
    )(table, asked)


def scatter_kernel(index_ref, value_ref, out_ref):
    sources = index_ref.shape[0]
    high_count = out_ref.shape[0] // 3
    tiles = low_tiles()
    high_iota = lax.broadcasted_iota(jnp.int32, (high_count, 128), 0)
    group = min(64, sources)

    def add_group(i, total):
        start = pl.multiple_of(i * group, group)
        block = index_ref[pl.ds(start, group), :]
        hot = []
        spread = []
        for s in range(group):
            row = block[s : s + 1, :]
            hot.append(hot_low(row & (LOW - 1), tiles))
            mine = high_iota == row // LOW
            values = value_ref[start + s]
            first = values.astype(BF16).astype(F32)
            rows = []
            for part in (first, values - first):
                for q in range(3):
                    rows.append(jnp.where(mine, part[q : q + 1], 0.0))
            spread.append(jnp.concatenate(rows, axis=0).astype(BF16))
        sums = lax.dot_general(
            jnp.concatenate(spread, axis=1),
            jnp.concatenate(hot, axis=1),
            (((1,), (1,)), ((), ())),
            preferred_element_type=F32,
        )
        return total + (sums[: 3 * high_count] + sums[3 * high_count :])

    out_ref[...] = lax.fori_loop(
        0, sources // group, add_group, jnp.zeros(out_ref.shape, F32)
    )


def scatter(asked, values, high_count):
    return pl.pallas_call(
        scatter_kernel,
        out_shape=jax.ShapeDtypeStruct((3 * high_count, LOW), F32),
        compiler_params=ROOM,
        name="scatter",
    )(asked, values)


LANE_GATHER = lax.GatherDimensionNumbers(
    offset_dims=(),
    collapsed_slice_dims=(1,),
    start_index_map=(1,),
    operand_batching_dims=(0,),
    start_indices_batching_dims=(0,),
)


def lanes_at(values, lanes):
    return lax.gather(
        values,
        lanes[..., None],
        LANE_GATHER,
        slice_sizes=(1, 1),
        mode=lax.GatherScatterMode.PROMISE_IN_BOUNDS,
    )


def remap_kernel(
    near_ref, far_ref, place_ref, order_ref, weight_ref, class_ref, mask_ref,
    source_ref, total_ref, left_ref, right_ref, table_ref,
):
    width, row_count, cols = weight_ref.shape
    groups = near_ref.shape[0]
    classes = near_ref.shape[1] // 128

    answers = jnp.concatenate([near_ref[...], far_ref[...]], axis=0)
    both = []
    for parity in range(2):
        place = jnp.concatenate(
            [place_ref[groups * k : groups * (k + 1), :] for k in (parity, parity + 2)],
            axis=0,
        )
        both.append(
            lax.dot_general(
                place, answers, (((0,), (0,)), ((), ())), preferred_element_type=F32
            )
        )
    lower = lax.broadcasted_iota(jnp.int32, (row_count, 128), 1) < 64
    picked = []
    for e in range(0, classes, 2):
        here, there = [
            [array[:, 128 * c : 128 * c + 128] for array in both] for c in (e, e + 1)
        ]
        picked.append(
            jnp.where(
                lower,
                here[0] + pltpu.roll(here[1], 64, 1),
                pltpu.roll(there[0], 64, 1) + there[1],
            ).astype(BF16)
        )
    table_ref[...] = jnp.dot(
        jnp.concatenate(picked, axis=1), order_ref[...], preferred_element_type=F32
    ).astype(BF16)

    tile = min(32, row_count)

    def remap_rows(i, carry):
        rows = pl.ds(pl.multiple_of(i * tile, tile), tile)
        chosen = (class_ref[rows, :] * 8).astype(jnp.int16)
        total = jnp.zeros((tile, cols), F32)
        found = [jnp.zeros((tile, cols), F32)] * 2
        for g in range(width // 8):
            part = table_ref[rows, 128 * g : 128 * g + 128]
            for b in range(8):
                weight = weight_ref[8 * g + b, rows, :].astype(F32)
                value = lanes_at(part, chosen + jnp.asarray(b, jnp.int16)).astype(F32)
                found[b % 2] = found[b % 2] + weight * value
                total = total + weight
        total_ref[rows, :] = total
        source_ref[rows, :] = mask_ref[rows, :].astype(F32) * (
            (found[0] + found[1]) / total
        )
        return carry

    lax.fori_loop(0, row_count // tile, remap_rows, 0)

    lane = lax.broadcasted_iota(jnp.int32, (EDGE, cols), 1)
    line = lax.broadcasted_iota(jnp.int32, (EDGE, cols), 0)
    for out_ref, offset in ((left_ref, 0), (right_ref, cols - EDGE)):
        out_ref[...] = lax.dot_general(
            jnp.where(lane == line + offset, 1.0, 0.0),
            source_ref[...],
            (((1,), (1,)), ((), ())),
            precision=EXACT,
            preferred_element_type=F32,
        )


def remap(near, far, place, order, weights, classes, mask):
    row_count, cols = weights.shape[1:]
    plane = jax.ShapeDtypeStruct((row_count, cols), F32)
    edge = jax.ShapeDtypeStruct((EDGE, row_count), F32)
    return pl.pallas_call(
        remap_kernel,
        out_shape=(plane, plane, edge, edge),
        scratch_shapes=[pltpu.VMEM((row_count, order.shape[1]), BF16)],
        compiler_params=ROOM,
        name="remap",
    )(near, far, place, order, weights, classes, mask)


def side_kernel(source_ref, low_ref, high_ref, side_ref, top_ref, bottom_ref):
    row_count, cols = source_ref.shape
    lane = lax.broadcasted_iota(jnp.int32, (2 * EDGE, cols), 1)
    line = lax.broadcasted_iota(jnp.int32, (2 * EDGE, cols), 0)
    spot = jnp.where(line < EDGE, line, line + cols - 2 * EDGE)
    side = lax.dot_general(
        jnp.concatenate([high_ref[...], low_ref[...]], axis=0),
        jnp.where(lane == spot, 1.0, 0.0),
        (((0,), (0,)), ((), ())),
        precision=EXACT,
        preferred_element_type=F32,
    )
    side_ref[...] = side
    for out_ref, first in ((top_ref, 0), (bottom_ref, row_count - EDGE)):
        out_ref[:, :cols] = source_ref[first : first + EDGE, :]
        out_ref[:, cols:] = side[first : first + EDGE, :]


def side(source, from_low, from_high):
    row_count, cols = source.shape
    return pl.pallas_call(
        side_kernel,
        out_shape=(
            jax.ShapeDtypeStruct((row_count, cols), F32),
            jax.ShapeDtypeStruct((EDGE, 2 * cols), F32),
            jax.ShapeDtypeStruct((EDGE, 2 * cols), F32),
        ),
        compiler_params=ROOM,
        name="side",
    )(source, from_low, from_high)


def relax_kernel(
    source_ref, side_ref, above_ref, below_ref, fixed_ref, inside_ref, total_ref, mask_ref,
    thick_ref, field_ref,
):
    row_count, cols = source_ref.shape
    rows, lanes = inside_ref.shape
    ahead = lambda a, axis: pltpu.roll(a, (rows, lanes)[axis] - 1, axis)
    back = lambda a, axis: pltpu.roll(a, 1, axis)
    source = SMB_RATE * jnp.concatenate(
        [
            above_ref[...],
            jnp.concatenate([source_ref[...], side_ref[...]], axis=1),
            below_ref[...],
        ],
        axis=0,
    )
    bed, diff, thick = fixed_ref[0], fixed_ref[1], fixed_ref[2]
    inside = inside_ref[...]
    gain = [0.5 * (diff + ahead(diff, axis)) for axis in range(2)]
    for step in range(STEPS):
        surface = bed + thick
        change = source
        for axis in range(2):
            flow = gain[axis] * (ahead(surface, axis) - surface)
            change = change + (flow - back(flow, axis))
        thick = jnp.maximum(thick + change, 0.0) * inside
    own = thick[EDGE : EDGE + row_count, :cols]
    thick_ref[...] = own
    total = total_ref[...]
    field_ref[0] = ((bed[EDGE : EDGE + row_count, :cols] + own) / total).astype(BF16)
    field_ref[1] = (mask_ref[...].astype(F32) * jnp.minimum(own, 1.0) / total).astype(BF16)
    field_ref[2] = (1.0 / total).astype(BF16)


def relax(source, side_tile, above, below, fixed, inside, total, mask):
    return pl.pallas_call(
        relax_kernel,
        out_shape=(
            jax.ShapeDtypeStruct(source.shape, F32),
            jax.ShapeDtypeStruct((3,) + source.shape, BF16),
        ),
        compiler_params=ROOM,
        name="relax",
    )(source, side_tile, above, below, fixed, inside, total, mask)


def per_device(
    fluxes, weights, land_rows, owners, elev_class, ice_mask, bed, thickness, diffusivity
):
    groups = lax.axis_size("gx") * lax.axis_size("gy")
    is_ice = lax.axis_index("grp") == 1
    block_weights = weights[0]
    width, row_count, cols = block_weights.shape
    classes, cells = fluxes.shape[1:]
    high_count = cells // LOW

    low_half, high_half, place = head(
        owners.reshape(1, row_count), jnp.transpose(land_rows[0]), groups
    )
    request = jnp.where(is_ice, low_half, swap_cores(high_half))
    asked = lax.all_to_all(request, PLANES, split_axis=0, concat_axis=0, tiled=True)

    flux, fixed = lax.optimization_barrier(
        (fluxes[0], jnp.stack([bed[0], diffusivity[0], thickness[0]]), request)
    )[:2]
    table = jnp.pad(flux.astype(BF16), ((0, 16 - classes), (0, 0)))
    table = jnp.transpose(table.reshape(16, high_count, LOW), (1, 0, 2)).reshape(-1, LOW)
    table = jnp.where(is_ice, swap_cores(table), table)
    turn = lambda part: jnp.transpose(part, (0, 2, 1))
    from_low = turn(ring(turn(fixed[:, :, cols - STEPS :]), "gy", 1))
    from_high = turn(ring(turn(fixed[:, :, :STEPS]), "gy", -1))
    fixed = jnp.concatenate(
        [fixed, from_high, jnp.zeros((3, row_count, cols - 2 * STEPS), F32), from_low], axis=2
    )

    row_at = lax.broadcasted_iota(jnp.int32, (row_count + 2 * EDGE, 2 * cols), 0) - EDGE
    col_at = lax.broadcasted_iota(jnp.int32, (row_count + 2 * EDGE, 2 * cols), 1)
    col_at = jnp.where(col_at < cols + cols // 2, col_at, col_at - 2 * cols)
    at_x, at_y = lax.axis_index("gx"), lax.axis_index("gy")
    inside = (
        ((row_at >= 0) | (at_x > 0))
        & ((row_at < row_count) | (at_x < lax.axis_size("gx") - 1))
        & ((col_at >= 0) | (at_y > 0))
        & ((col_at < cols) | (at_y < lax.axis_size("gy") - 1))
    ).astype(F32)
    line = lax.broadcasted_iota(jnp.int32, (classes * width, 16 * width), 0)
    lane = lax.broadcasted_iota(jnp.int32, (classes * width, 16 * width), 1)
    order = (
        (lane // 128 == line % width // 8)
        & (lane % 128 // 8 == line // width)
        & (lane % 8 == line % 8)
    ).astype(BF16)

    asked, fixed, order, inside = lax.optimization_barrier((asked, fixed, order, inside))
    answer = pick(table, asked, classes)
    near = lax.all_to_all(answer, PLANES, split_axis=0, concat_axis=0, tiled=True)

    fixed = after(fixed, answer)
    above = ring(fixed[:, row_count - EDGE :], "gx", 1)
    below = ring(fixed[:, :EDGE], "gx", -1)
    fixed = jnp.concatenate([above, fixed, below], axis=1) * inside
    near, fixed = lax.optimization_barrier((near, fixed))

    near = near.reshape(groups, classes * 128)
    source, total, left, right = remap(
        near, swap_cores(near), place, order, block_weights, elev_class[0], ice_mask[0]
    )
    side_tile, top, bottom = side(source, ring(right, "gy", 1), ring(left, "gy", -1))
    thick, fields = relax(
        source,
        side_tile,
        ring(bottom, "gx", 1),
        ring(top, "gx", -1),
        fixed,
        inside,
        total,
        ice_mask[0],
    )

    partial = jnp.einsum("brj,qrj->qrb", block_weights, fields, preferred_element_type=F32)
    outgoing = jnp.einsum(
        "kor,qrb->koqb",
        place.reshape(4, groups, row_count).astype(F32),
        partial,
        precision=EXACT,
        preferred_element_type=F32,
    )
    outgoing = [jnp.concatenate([outgoing[k], outgoing[k + 1]], axis=2) for k in (0, 2)]
    sent = jnp.where(is_ice, outgoing[0], swap_cores(outgoing[1]))
    arrived = lax.all_to_all(sent, PLANES, split_axis=0, concat_axis=0, tiled=True)
    land_sums = scatter(asked, arrived, high_count)
    land_sums = (land_sums + swap_cores(land_sums)).reshape(3, cells)
    averaged = land_sums[:2] / jnp.maximum(land_sums[2], 1.0)
    land_fields = jnp.where(is_ice, 0.0, averaged)[None]
    thickness_new = jnp.where(is_ice, thick, 0.0)[None]
    return (land_fields, thickness_new)


def solution(mesh):
    return jax.shard_map(
        per_device,
        mesh=mesh,
        in_specs=(
            P("grp", None, ("gx", "gy")),
            P("grp", None, "gx", "gy"),
            P("grp", "gx", "gy"),
            P("grp", "gx", "gy", None, None),
            P("grp", "gx", "gy"),
            P("grp", "gx", "gy"),
            P("grp", "gx", "gy"),
            P("grp", "gx", "gy"),
            P("grp", "gx", "gy"),
        ),
        out_specs=(P("grp", None, ("gx", "gy")), P("grp", "gx", "gy")),
        check_vma=False,
    )
```

```python
import jax
import jax.numpy as jnp
from jax import lax
from jax.experimental import pallas as pl
from jax.experimental.pallas import tpu as pltpu
from jax.sharding import PartitionSpec as P


STEPS = 4
SMB_RATE = 0.5
LOW = 256
EDGE = 8
PLANES = ("gx", "gy")
F32 = jnp.float32
BF16 = jnp.bfloat16
EXACT = lax.Precision.HIGHEST
COST = pl.CostEstimate(flops=0, transcendentals=0, bytes_accessed=12 << 20)
ROOM = pltpu.CompilerParams(vmem_limit_bytes=16 << 20)
ON_CHIP = pl.BlockSpec(memory_space=pltpu.VMEM)
SCALARS = pl.BlockSpec(memory_space=pltpu.SMEM)


def swap_cores(value):
    return lax.ppermute(value, "grp", [(0, 1), (1, 0)])


def trade(value, axis, phase):
    count = lax.axis_size(axis)
    pairs = []
    for i in range(count):
        other = i + 1 if i % 2 == phase else i - 1
        pairs.append((i, other if 0 <= other < count else i))
    return lax.ppermute(value, axis, pairs)


def trade_both(first, second, axis):
    return trade(first, axis, 0), trade(second, axis, 1)


def ones_where(mask):
    return jnp.where(mask, 1.0, 0.0).astype(BF16)


def head_kernel(owner_ref, rows_ref, low_ref, high_ref, place_ref):
    groups, row_count = low_ref.shape[0], owner_ref.shape[1]
    width = rows_ref.shape[0]
    named = lax.broadcasted_iota(jnp.int32, (groups, row_count), 0) == owner_ref[...]
    square = (row_count, row_count)
    earlier = lax.broadcasted_iota(jnp.int32, square, 0) < lax.broadcasted_iota(
        jnp.int32, square, 1
    )
    rank = jnp.dot(ones_where(named), ones_where(earlier), preferred_element_type=F32)
    rank = jnp.where(named, rank, -1.0)
    rows = rows_ref[...]
    digits = jnp.concatenate([rows >> 3, rows & 7], axis=0).astype(F32).astype(BF16)
    for half, out_ref in enumerate((low_ref, high_ref)):
        parts = []
        for k in (2 * half, 2 * half + 1):
            mine = ones_where(rank == k)
            place_ref[groups * k : groups * (k + 1), :] = mine
            found = lax.dot_general(
                mine, digits, (((1,), (1,)), ((), ())), preferred_element_type=F32
            )
            parts.append(8.0 * found[:, :width] + found[:, width:])
        out_ref[...] = jnp.concatenate(parts, axis=1).astype(jnp.int32)


def head(owner_row, rows, groups):
    row_count = owner_row.shape[1]
    lanes = 2 * rows.shape[0]
    return pl.pallas_call(
        head_kernel,
        out_shape=(
            jax.ShapeDtypeStruct((groups, lanes), jnp.int32),
            jax.ShapeDtypeStruct((groups, lanes), jnp.int32),
            jax.ShapeDtypeStruct((4 * groups, row_count), BF16),
        ),
        compiler_params=ROOM,
        cost_estimate=COST,
        name="head",
    )(owner_row, rows)


def hot_low(low, tiles):
    key = jnp.broadcast_to(low.astype(F32), (16, 128)).astype(BF16)
    one = jnp.ones((16, 128), BF16)
    zero = jnp.zeros((16, 128), BF16)
    return jnp.concatenate([jnp.where(tile == key, one, zero) for tile in tiles], axis=0)


def low_tiles():
    base = lax.broadcasted_iota(jnp.int32, (16, 128), 0)
    return [(base + 16 * i).astype(F32).astype(BF16) for i in range(LOW // 16)]


def pick_kernel(table_ref, index_ref, out_ref):
    sources = index_ref.shape[0]
    high_count = table_ref.shape[0] // 16
    table = table_ref[...]
    tiles = low_tiles()
    group = min(32, sources)

    def pick_group(i, carry):
        start = pl.multiple_of(i * group, group)
        block = index_ref[pl.ds(start, group), :]
        for s in range(0, group, 2):
            rows = [block[s + d : s + d + 1, :] for d in range(2)]
            hot = jnp.concatenate([hot_low(row & (LOW - 1), tiles) for row in rows], axis=1)
            found = jnp.dot(table, hot, preferred_element_type=F32)
            for d in range(2):
                high = jnp.broadcast_to(rows[d] // LOW, (16, 128))
                part = found[:, 128 * d : 128 * d + 128]
                total = part[:16]
                for h in range(1, high_count):
                    total = jnp.where(high == h, part[16 * h : 16 * h + 16], total)
                total = total.astype(BF16)
                for pair in range(out_ref.shape[1]):
                    out_ref[start + s + d, pair] = total[2 * pair : 2 * pair + 2]
        return carry

    lax.fori_loop(0, sources // group, pick_group, 0)


def pick(table, asked, classes):
    return pl.pallas_call(
        pick_kernel,
        out_shape=jax.ShapeDtypeStruct((asked.shape[0], classes // 2, 2, 128), BF16),
        compiler_params=ROOM,
        cost_estimate=COST,
        name="pick",
    )(table, asked)


def scatter_kernel(index_ref, value_ref, out_ref):
    sources = index_ref.shape[0]
    high_count = out_ref.shape[0] // 3
    tiles = low_tiles()
    high_iota = lax.broadcasted_iota(jnp.int32, (high_count, 128), 0)
    group = min(64, sources)

    def add_group(i, total):
        start = pl.multiple_of(i * group, group)
        block = index_ref[pl.ds(start, group), :]
        hot = []
        spread = []
        for s in range(group):
            row = block[s : s + 1, :]
            hot.append(hot_low(row & (LOW - 1), tiles))
            mine = high_iota == row // LOW
            values = value_ref[pl.ds(3 * start + 3 * s, 3), :]
            first = values.astype(BF16).astype(F32)
            rows = []
            for part in (first, values - first):
                for q in range(3):
                    rows.append(jnp.where(mine, part[q : q + 1], 0.0))
            spread.append(jnp.concatenate(rows, axis=0).astype(BF16))
        sums = lax.dot_general(
            jnp.concatenate(spread, axis=1),
            jnp.concatenate(hot, axis=1),
            (((1,), (1,)), ((), ())),
            preferred_element_type=F32,
        )
        return total + (sums[: 3 * high_count] + sums[3 * high_count :])

    out_ref[...] = lax.fori_loop(
        0, sources // group, add_group, jnp.zeros(out_ref.shape, F32)
    )


def scatter(asked, values, high_count):
    return pl.pallas_call(
        scatter_kernel,
        out_shape=jax.ShapeDtypeStruct((3 * high_count, LOW), F32),
        compiler_params=ROOM,
        cost_estimate=COST,
        name="scatter",
    )(asked, values)


LANE_GATHER = lax.GatherDimensionNumbers(
    offset_dims=(),
    collapsed_slice_dims=(1,),
    start_index_map=(1,),
    operand_batching_dims=(0,),
    start_indices_batching_dims=(0,),
)


def lanes_at(values, lanes):
    return lax.gather(
        values,
        lanes[..., None],
        LANE_GATHER,
        slice_sizes=(1, 1),
        mode=lax.GatherScatterMode.PROMISE_IN_BOUNDS,
    )


def cut_edges(odd_ref, plane, even_ref, other_ref):
    cols = plane.shape[1]
    lane = lax.broadcasted_iota(jnp.int32, (EDGE, cols), 1)
    line = lax.broadcasted_iota(jnp.int32, (EDGE, cols), 0)
    odd = odd_ref[0] == 1
    for out_ref, offset in (
        (even_ref, jnp.where(odd, 0, cols - EDGE)),
        (other_ref, jnp.where(odd, cols - EDGE, 0)),
    ):
        out_ref[...] = lax.dot_general(
            jnp.where(lane == line + offset, 1.0, 0.0),
            plane,
            (((1,), (1,)), ((), ())),
            precision=EXACT,
            preferred_element_type=F32,
        )


def table_kernel(near_ref, far_ref, place_ref, order_ref, table_ref):
    groups = near_ref.shape[0]
    row_count = table_ref.shape[0]
    classes = near_ref.shape[1] // 128

    answers = jnp.concatenate([near_ref[...], far_ref[...]], axis=0)
    both = []
    for parity in range(2):
        place = jnp.concatenate(
            [place_ref[groups * k : groups * (k + 1), :] for k in (parity, parity + 2)],
            axis=0,
        )
        both.append(
            lax.dot_general(
                place, answers, (((0,), (0,)), ((), ())), preferred_element_type=F32
            )
        )
    lower = lax.broadcasted_iota(jnp.int32, (row_count, 128), 1) < 64
    picked = []
    for e in range(0, classes, 2):
        here, there = [
            [array[:, 128 * c : 128 * c + 128] for array in both] for c in (e, e + 1)
        ]
        picked.append(
            jnp.where(
                lower,
                here[0] + pltpu.roll(here[1], 64, 1),
                pltpu.roll(there[0], 64, 1) + there[1],
            ).astype(BF16)
        )
    table_ref[...] = jnp.dot(
        jnp.concatenate(picked, axis=1), order_ref[...], preferred_element_type=F32
    ).astype(BF16)


def remap_kernel(
    odd_ref, table_ref, weight_ref, class_ref, mask_ref, source_ref, total_ref, even_ref, other_ref
):
    width, row_count, cols = weight_ref.shape
    tile = min(32, row_count)

    def remap_rows(i, carry):
        rows = pl.ds(pl.multiple_of(i * tile, tile), tile)
        chosen = (class_ref[rows, :] * 8).astype(jnp.int16)
        total = jnp.zeros((tile, cols), F32)
        found = [jnp.zeros((tile, cols), F32)] * 2
        for g in range(width // 8):
            part = table_ref[rows, 128 * g : 128 * g + 128]
            for b in range(8):
                weight = weight_ref[8 * g + b, rows, :].astype(F32)
                value = lanes_at(part, chosen + jnp.asarray(b, jnp.int16)).astype(F32)
                found[b % 2] = found[b % 2] + weight * value
                total = total + weight
        total_ref[rows, :] = total
        source_ref[rows, :] = mask_ref[rows, :].astype(F32) * (
            (found[0] + found[1]) / total
        )
        return carry

    lax.fori_loop(0, row_count // tile, remap_rows, 0)
    cut_edges(odd_ref, source_ref[...], even_ref, other_ref)


def remap(odd, near, far, place, order, weights, classes, mask):
    row_count, cols = weights.shape[1:]
    table = pl.pallas_call(
        table_kernel,
        in_specs=[ON_CHIP] * 4,
        out_specs=ON_CHIP,
        out_shape=jax.ShapeDtypeStruct((row_count, order.shape[1]), BF16),
        compiler_params=ROOM,
        cost_estimate=COST,
        name="table",
    )(near, far, place, order)
    edge = jax.ShapeDtypeStruct((EDGE, row_count), F32)
    plane = jax.ShapeDtypeStruct((row_count, cols), F32)
    return pl.pallas_call(
        remap_kernel,
        in_specs=[SCALARS] + [ON_CHIP] * 4,
        out_specs=[ON_CHIP] * 4,
        out_shape=(plane, plane, edge, edge),
        compiler_params=ROOM,
        cost_estimate=COST,
        name="remap",
    )(odd, table, weights, classes, mask)


def side_kernel(
    odd_ref, source_ref, bed_ref, diff_ref, thick_ref, even_ref, other_ref, fixed_even_ref,
    fixed_other_ref, side_ref, send_ref, send_other_ref,
):
    row_count, cols = source_ref.shape
    lane = lax.broadcasted_iota(jnp.int32, (2 * EDGE, cols), 1)
    line = lax.broadcasted_iota(jnp.int32, (2 * EDGE, cols), 0)
    line = jnp.where(odd_ref[0] == 1, (line + EDGE) % (2 * EDGE), line)
    spot = jnp.where(line < EDGE, line, line + cols - 2 * EDGE)
    spread = jnp.where(lane == spot, 1.0, 0.0)
    odd = odd_ref[1] == 1
    for p, plane_ref in enumerate((source_ref, bed_ref, diff_ref, thick_ref)):
        if p == 0:
            edges = [even_ref[...], other_ref[...]]
        else:
            edges = [fixed_even_ref[p - 1], fixed_other_ref[p - 1]]
        side = lax.dot_general(
            jnp.concatenate(edges, axis=0),
            spread,
            (((0,), (0,)), ((), ())),
            precision=EXACT,
            preferred_element_type=F32,
        )
        side_ref[p] = side
        first = jnp.concatenate([plane_ref[:EDGE, :], side[:EDGE]], axis=1)
        last = jnp.concatenate(
            [plane_ref[row_count - EDGE :, :], side[row_count - EDGE :]], axis=1
        )
        send_ref[p] = jnp.where(odd, first, last)
        send_other_ref[p] = jnp.where(odd, last, first)


def side(odd, source, bed, diff, thick, edges, fixed_edges):
    row_count, cols = source.shape
    strip = jax.ShapeDtypeStruct((4, EDGE, 2 * cols), F32)
    return pl.pallas_call(
        side_kernel,
        in_specs=[SCALARS] + [ON_CHIP] * 8,
        out_specs=[ON_CHIP] * 3,
        out_shape=(jax.ShapeDtypeStruct((4, row_count, cols), F32), strip, strip),
        compiler_params=ROOM,
        cost_estimate=COST,
        name="side",
    )(odd, source, bed, diff, thick, *edges, *fixed_edges)


def relax_kernel(
    odd_ref, source_ref, bed_ref, diff_ref, start_ref, side_ref, even_ref, other_ref,
    inside_ref, total_ref, mask_ref, thick_ref, field_ref,
):
    row_count, cols = source_ref.shape
    rows, lanes = inside_ref.shape
    ahead = lambda a, axis: pltpu.roll(a, (rows, lanes)[axis] - 1, axis)
    back = lambda a, axis: pltpu.roll(a, 1, axis)
    inside = inside_ref[...]
    odd = odd_ref[1] == 1
    planes = []
    for p, plane_ref in enumerate((source_ref, bed_ref, diff_ref, start_ref)):
        even, other = even_ref[p], other_ref[p]
        planes.append(
            inside
            * jnp.concatenate(
                [
                    jnp.where(odd, even, other),
                    jnp.concatenate([plane_ref[...], side_ref[p]], axis=1),
                    jnp.where(odd, other, even),
                ],
                axis=0,
            )
        )
    source, bed, diff, thick = planes
    source = SMB_RATE * source
    gain = [0.5 * (diff + ahead(diff, axis)) for axis in range(2)]
    for _ in range(STEPS):
        surface = bed + thick
        change = source
        for axis in range(2):
            flow = gain[axis] * (ahead(surface, axis) - surface)
            change = change + (flow - back(flow, axis))
        thick = jnp.maximum(thick + change, 0.0) * inside
    own = thick[EDGE : EDGE + row_count, :cols]
    thick_ref[...] = own
    total = total_ref[...]
    field_ref[0] = ((bed_ref[...] + own) / total).astype(BF16)
    field_ref[1] = (mask_ref[...].astype(F32) * jnp.minimum(own, 1.0) / total).astype(BF16)
    field_ref[2] = (1.0 / total).astype(BF16)


def relax(odd, source, bed, diff, thick, sides, strips, inside, total, mask):
    return pl.pallas_call(
        relax_kernel,
        in_specs=[SCALARS] + [ON_CHIP] * 10,
        out_specs=[ON_CHIP] * 2,
        out_shape=(
            jax.ShapeDtypeStruct(source.shape, F32),
            jax.ShapeDtypeStruct((3,) + source.shape, BF16),
        ),
        compiler_params=ROOM,
        cost_estimate=COST,
        name="relax",
    )(odd, source, bed, diff, thick, sides, *strips, inside, total, mask)


def coupled(
    fluxes, weights, land_rows, owners, elev_class, ice_mask, bed, thickness, diffusivity
):
    groups = lax.axis_size("gx") * lax.axis_size("gy")
    is_ice = lax.axis_index("grp") == 1
    block_weights = weights[0]
    width, row_count, cols = block_weights.shape
    classes, cells = fluxes.shape[1:]
    high_count = cells // LOW

    low_half, high_half, place = head(
        owners.reshape(1, row_count), jnp.transpose(land_rows[0]), groups
    )
    request = jnp.where(is_ice, low_half, swap_cores(high_half))
    asked = lax.all_to_all(request, PLANES, split_axis=0, concat_axis=0, tiled=True)

    flux, bed_now, diff_now, thick_now = lax.optimization_barrier(
        (fluxes[0], bed[0], diffusivity[0], thickness[0], request)
    )[:4]
    table = jnp.pad(flux.astype(BF16), ((0, 16 - classes), (0, 0)))
    table = jnp.transpose(table.reshape(16, high_count, LOW), (1, 0, 2)).reshape(-1, LOW)
    other_table = swap_cores(table)
    table = jnp.where(is_ice, other_table, table)
    at_x, at_y = lax.axis_index("gx"), lax.axis_index("gy")
    odd = jnp.stack([at_y % 2, at_x % 2]).astype(jnp.int32)
    turn = lambda cut: jnp.stack([jnp.transpose(a[:, cut]) for a in (bed_now, diff_now, thick_now)])
    first, last = turn(slice(0, EDGE)), turn(slice(cols - EDGE, cols))
    fixed_edges = [jnp.where(odd[0] == 1, first, last), jnp.where(odd[0] == 1, last, first)]

    row_at = lax.broadcasted_iota(jnp.int32, (row_count + 2 * EDGE, 2 * cols), 0) - EDGE
    col_at = lax.broadcasted_iota(jnp.int32, (row_count + 2 * EDGE, 2 * cols), 1)
    col_at = jnp.where(col_at < cols + cols // 2, col_at, col_at - 2 * cols)
    inside = (
        ((row_at >= 0) | (at_x > 0))
        & ((row_at < row_count) | (at_x < lax.axis_size("gx") - 1))
        & ((col_at >= 0) | (at_y > 0))
        & ((col_at < cols) | (at_y < lax.axis_size("gy") - 1))
    ).astype(F32)
    line = lax.broadcasted_iota(jnp.int32, (classes * width, 16 * width), 0)
    lane = lax.broadcasted_iota(jnp.int32, (classes * width, 16 * width), 1)
    source_line = ((lane & 127) >> 3) * width + (lane >> 7) * 8 + (lane & 7)
    order = (source_line == line).astype(BF16)

    asked, order, inside, *fixed_edges = lax.optimization_barrier(
        (asked, order, inside, *fixed_edges)
    )
    answer = pick(table, asked, classes)
    near = lax.all_to_all(answer, PLANES, split_axis=0, concat_axis=0, tiled=True)
    fixed_edges = trade_both(*fixed_edges, "gy")
    near, *fixed_edges = lax.optimization_barrier((near, *fixed_edges))

    near = near.reshape(groups, classes * 128)
    source, total, *edges = remap(
        odd, near, swap_cores(near), place, order, block_weights, elev_class[0], ice_mask[0]
    )
    sides, *strips = side(
        odd, source, bed[0], diffusivity[0], thickness[0], trade_both(*edges, "gy"), fixed_edges
    )
    strips = trade_both(*strips, "gx")
    thick, fields = relax(
        odd, source, bed[0], diffusivity[0], thickness[0], sides, strips, inside, total,
        ice_mask[0],
    )

    partial = jnp.einsum("brj,qrj->qrb", block_weights, fields, preferred_element_type=F32)
    outgoing = jnp.einsum(
        "kor,qrb->koqb",
        place.reshape(4, groups, row_count).astype(F32),
        partial,
        precision=EXACT,
        preferred_element_type=F32,
    )
    outgoing = [jnp.concatenate([outgoing[k], outgoing[k + 1]], axis=2) for k in (0, 2)]
    sent = jnp.where(is_ice, outgoing[0], swap_cores(outgoing[1]))
    arrived = lax.all_to_all(
        sent.reshape(groups, -1), PLANES, split_axis=0, concat_axis=0, tiled=True
    )
    land_sums = scatter(asked, arrived.reshape(3 * groups, 128), high_count)
    land_sums = (land_sums + swap_cores(land_sums)).reshape(3, cells)
    averaged = land_sums[:2] / jnp.maximum(land_sums[2], 1.0)
    land_fields = jnp.where(is_ice, 0.0, averaged)[None]
    thickness_new = jnp.where(is_ice, thick, 0.0)[None]
    return (land_fields, thickness_new)


def solution(mesh):
    return jax.shard_map(
        coupled,
        mesh=mesh,
        in_specs=(
            P("grp", None, ("gx", "gy")),
            P("grp", None, "gx", "gy"),
            P("grp", "gx", "gy"),
            P("grp", "gx", "gy", None, None),
            P("grp", "gx", "gy"),
            P("grp", "gx", "gy"),
            P("grp", "gx", "gy"),
            P("grp", "gx", "gy"),
            P("grp", "gx", "gy"),
        ),
        out_specs=(P("grp", None, ("gx", "gy")), P("grp", "gx", "gy")),
        check_vma=False,
    )
```

```python
import jax
import jax.numpy as jnp
from jax import lax
from jax.experimental import pallas as pl
from jax.experimental.pallas import tpu as pltpu
from jax.sharding import PartitionSpec as P


STEPS = 4
SMB_RATE = 0.5
LOW = 256
EDGE = 8
PLANES = ("gx", "gy")
F32 = jnp.float32
BF16 = jnp.bfloat16
EXACT = lax.Precision.HIGHEST
COST = pl.CostEstimate(flops=0, transcendentals=0, bytes_accessed=12 << 20)
ROOM = pltpu.CompilerParams(vmem_limit_bytes=16 << 20)
IN_PLACE = pl.BlockSpec(memory_space=pltpu.HBM)
ON_CHIP = pl.BlockSpec(memory_space=pltpu.VMEM)
SCALARS = pl.BlockSpec(memory_space=pltpu.SMEM)


def swap_cores(value):
    return lax.ppermute(value, "grp", [(0, 1), (1, 0)])


def trade(value, axis, phase):
    count = lax.axis_size(axis)
    pairs = []
    for i in range(count):
        other = i + 1 if i % 2 == phase else i - 1
        pairs.append((i, other if 0 <= other < count else i))
    return lax.ppermute(value, axis, pairs)


def trade_both(first, second, axis):
    return trade(first, axis, 0), trade(second, axis, 1)


def ones_where(mask):
    return jnp.where(mask, 1.0, 0.0).astype(BF16)


def head_kernel(owner_hbm, rows_hbm, low_ref, high_ref, place_ref, owner_ref, rows_ref, done):
    loads = [
        pltpu.make_async_copy(owner_hbm, owner_ref, done.at[0]),
        pltpu.make_async_copy(rows_hbm, rows_ref, done.at[1]),
    ]
    for load in loads:
        load.start()
    for load in loads:
        load.wait()
    groups, row_count = low_ref.shape[0], owner_ref.shape[1]
    width = rows_ref.shape[0]
    named = lax.broadcasted_iota(jnp.int32, (groups, row_count), 0) == owner_ref[...]
    square = (row_count, row_count)
    earlier = lax.broadcasted_iota(jnp.int32, square, 0) < lax.broadcasted_iota(
        jnp.int32, square, 1
    )
    rank = jnp.dot(ones_where(named), ones_where(earlier), preferred_element_type=F32)
    rank = jnp.where(named, rank, -1.0)
    rows = rows_ref[...]
    digits = jnp.concatenate([rows >> 3, rows & 7], axis=0).astype(F32).astype(BF16)
    for half, out_ref in enumerate((low_ref, high_ref)):
        parts = []
        for k in (2 * half, 2 * half + 1):
            mine = ones_where(rank == k)
            place_ref[groups * k : groups * (k + 1), :] = mine
            found = lax.dot_general(
                mine, digits, (((1,), (1,)), ((), ())), preferred_element_type=F32
            )
            parts.append(8.0 * found[:, :width] + found[:, width:])
        out_ref[...] = jnp.concatenate(parts, axis=1).astype(jnp.int32)


def head(owner_row, rows, groups):
    row_count = owner_row.shape[1]
    lanes = 2 * rows.shape[0]
    owner_row, rows = [
        pltpu.with_memory_space_constraint(value, pltpu.HBM) for value in (owner_row, rows)
    ]
    return pl.pallas_call(
        head_kernel,
        in_specs=[IN_PLACE] * 2,
        scratch_shapes=[
            pltpu.VMEM(owner_row.shape, jnp.int32),
            pltpu.VMEM(rows.shape, jnp.int32),
            pltpu.SemaphoreType.DMA((2,)),
        ],
        out_shape=(
            jax.ShapeDtypeStruct((groups, lanes), jnp.int32),
            jax.ShapeDtypeStruct((groups, lanes), jnp.int32),
            jax.ShapeDtypeStruct((4 * groups, row_count), BF16),
        ),
        compiler_params=ROOM,
        cost_estimate=COST,
        name="head",
    )(owner_row, rows)


def hot_low(low, tiles):
    key = jnp.broadcast_to(low.astype(F32), (16, 128)).astype(BF16)
    one = jnp.ones((16, 128), BF16)
    zero = jnp.zeros((16, 128), BF16)
    return jnp.concatenate([jnp.where(tile == key, one, zero) for tile in tiles], axis=0)


def low_tiles():
    base = lax.broadcasted_iota(jnp.int32, (16, 128), 0)
    return [(base + 16 * i).astype(F32).astype(BF16) for i in range(LOW // 16)]


def pick_kernel(table_ref, index_ref, out_ref):
    sources = index_ref.shape[0]
    high_count = table_ref.shape[0] // 16
    table = table_ref[...]
    tiles = low_tiles()
    group = min(64, sources)

    def pick_group(i, carry):
        start = pl.multiple_of(i * group, group)
        block = index_ref[pl.ds(start, group), :]
        for s in range(0, group, 2):
            rows = [block[s + d : s + d + 1, :] for d in range(2)]
            hot = jnp.concatenate([hot_low(row & (LOW - 1), tiles) for row in rows], axis=1)
            found = jnp.dot(table, hot, preferred_element_type=F32)
            for d in range(2):
                high = jnp.broadcast_to(rows[d] // LOW, (16, 128))
                part = found[:, 128 * d : 128 * d + 128]
                total = part[:16]
                for h in range(1, high_count):
                    total = jnp.where(high == h, part[16 * h : 16 * h + 16], total)
                total = total.astype(BF16)
                for pair in range(out_ref.shape[1]):
                    out_ref[start + s + d, pair] = total[2 * pair : 2 * pair + 2]
        return carry

    lax.fori_loop(0, sources // group, pick_group, 0)


def pick(table, asked, classes):
    return pl.pallas_call(
        pick_kernel,
        out_shape=jax.ShapeDtypeStruct((asked.shape[0], classes // 2, 2, 128), BF16),
        compiler_params=ROOM,
        cost_estimate=COST,
        name="pick",
    )(table, asked)


def scatter_kernel(index_ref, value_ref, out_ref):
    sources = index_ref.shape[0]
    high_count = out_ref.shape[0] // 3
    tiles = low_tiles()
    high_iota = lax.broadcasted_iota(jnp.int32, (high_count, 128), 0)
    group = min(64, sources)

    def add_group(i, total):
        start = pl.multiple_of(i * group, group)
        block = index_ref[pl.ds(start, group), :]
        hot = []
        spread = []
        for s in range(group):
            row = block[s : s + 1, :]
            hot.append(hot_low(row & (LOW - 1), tiles))
            mine = high_iota == row // LOW
            values = value_ref[pl.ds(3 * start + 3 * s, 3), :]
            first = values.astype(BF16).astype(F32)
            rows = []
            for part in (first, values - first):
                for q in range(3):
                    rows.append(jnp.where(mine, part[q : q + 1], 0.0))
            spread.append(jnp.concatenate(rows, axis=0).astype(BF16))
        sums = lax.dot_general(
            jnp.concatenate(spread, axis=1),
            jnp.concatenate(hot, axis=1),
            (((1,), (1,)), ((), ())),
            preferred_element_type=F32,
        )
        return total + (sums[: 3 * high_count] + sums[3 * high_count :])

    out_ref[...] = lax.fori_loop(
        0, sources // group, add_group, jnp.zeros(out_ref.shape, F32)
    )


def scatter(asked, values, high_count):
    return pl.pallas_call(
        scatter_kernel,
        out_shape=jax.ShapeDtypeStruct((3 * high_count, LOW), F32),
        compiler_params=ROOM,
        cost_estimate=COST,
        name="scatter",
    )(asked, values)


LANE_GATHER = lax.GatherDimensionNumbers(
    offset_dims=(),
    collapsed_slice_dims=(1,),
    start_index_map=(1,),
    operand_batching_dims=(0,),
    start_indices_batching_dims=(0,),
)


def lanes_at(values, lanes):
    return lax.gather(
        values,
        lanes[..., None],
        LANE_GATHER,
        slice_sizes=(1, 1),
        mode=lax.GatherScatterMode.PROMISE_IN_BOUNDS,
    )


def cut_edges(odd_ref, plane, even_ref, other_ref):
    cols = plane.shape[1]
    lane = lax.broadcasted_iota(jnp.int32, (EDGE, cols), 1)
    line = lax.broadcasted_iota(jnp.int32, (EDGE, cols), 0)
    odd = odd_ref[0] == 1
    for out_ref, offset in (
        (even_ref, jnp.where(odd, 0, cols - EDGE)),
        (other_ref, jnp.where(odd, cols - EDGE, 0)),
    ):
        out_ref[...] = lax.dot_general(
            jnp.where(lane == line + offset, 1.0, 0.0),
            plane,
            (((1,), (1,)), ((), ())),
            precision=EXACT,
            preferred_element_type=F32,
        )


def remap_kernel(
    odd_ref, near_ref, far_ref, place_ref, order_ref, weight_hbm, class_ref, mask_ref,
    fixed_even_ref, fixed_other_ref, source_ref, total_ref, even_ref, other_ref, table_ref, weight_ref, done,
):
    even_ref[1:] = fixed_even_ref[...]
    other_ref[1:] = fixed_other_ref[...]
    width, row_count, cols = weight_ref.shape
    tile = row_count // done.shape[0]

    def load(i):
        rows = pl.ds(pl.multiple_of(i * tile, tile), tile)
        return pltpu.make_async_copy(
            weight_hbm.at[:, rows, :], weight_ref.at[:, rows, :], done.at[i]
        )

    def start_load(i, carry):
        load(i).start()
        return carry

    lax.fori_loop(0, done.shape[0], start_load, 0)
    groups = near_ref.shape[0]
    classes = near_ref.shape[1] // 128

    answers = jnp.concatenate([near_ref[...], far_ref[...]], axis=0)
    both = []
    for parity in range(2):
        place = jnp.concatenate(
            [place_ref[groups * k : groups * (k + 1), :] for k in (parity, parity + 2)],
            axis=0,
        )
        both.append(
            lax.dot_general(
                place, answers, (((0,), (0,)), ((), ())), preferred_element_type=F32
            )
        )
    lower = lax.broadcasted_iota(jnp.int32, (row_count, 128), 1) < 64
    picked = []
    for e in range(0, classes, 2):
        here, there = [
            [array[:, 128 * c : 128 * c + 128] for array in both] for c in (e, e + 1)
        ]
        picked.append(
            jnp.where(
                lower,
                here[0] + pltpu.roll(here[1], 64, 1),
                pltpu.roll(there[0], 64, 1) + there[1],
            ).astype(BF16)
        )
    table_ref[...] = jnp.dot(
        jnp.concatenate(picked, axis=1), order_ref[...], preferred_element_type=F32
    ).astype(BF16)

    def remap_rows(i, carry):
        load(i).wait()
        rows = pl.ds(pl.multiple_of(i * tile, tile), tile)
        chosen = (class_ref[rows, :] * 8).astype(jnp.int16)
        total = jnp.zeros((tile, cols), F32)
        found = [jnp.zeros((tile, cols), F32)] * 2
        for g in range(width // 8):
            part = table_ref[rows, 128 * g : 128 * g + 128]
            for b in range(8):
                weight = weight_ref[8 * g + b, rows, :].astype(F32)
                value = lanes_at(part, chosen + jnp.asarray(b, jnp.int16)).astype(F32)
                found[b % 2] = found[b % 2] + weight * value
                total = total + weight
        total_ref[rows, :] = total
        source_ref[rows, :] = mask_ref[rows, :].astype(F32) * (
            (found[0] + found[1]) / total
        )
        return carry

    lax.fori_loop(0, row_count // tile, remap_rows, 0)
    cut_edges(odd_ref, source_ref[...], even_ref.at[0], other_ref.at[0])


def remap(odd, near, far, place, order, weights, classes, mask, fixed_edges):
    row_count, cols = weights.shape[1:]
    edge = jax.ShapeDtypeStruct((4, EDGE, row_count), F32)
    plane = jax.ShapeDtypeStruct((row_count, cols), F32)
    weights = pltpu.with_memory_space_constraint(weights, pltpu.HBM)
    return pl.pallas_call(
        remap_kernel,
        in_specs=[SCALARS] + [ON_CHIP] * 4 + [IN_PLACE] + [ON_CHIP] * 4,
        out_specs=[ON_CHIP] * 4,
        out_shape=(plane, plane, edge, edge),
        scratch_shapes=[
            pltpu.VMEM((row_count, order.shape[1]), BF16),
            pltpu.VMEM(weights.shape, BF16),
            pltpu.SemaphoreType.DMA((row_count // 32,)),
        ],
        compiler_params=ROOM,
        cost_estimate=COST,
        name="remap",
    )(odd, near, far, place, order, weights, classes, mask, *fixed_edges)


def side_kernel(
    odd_ref, source_ref, bed_ref, diff_ref, thick_ref, even_ref, other_ref,
    side_ref, send_ref, send_other_ref,
):
    row_count, cols = source_ref.shape
    lane = lax.broadcasted_iota(jnp.int32, (2 * EDGE, cols), 1)
    line = lax.broadcasted_iota(jnp.int32, (2 * EDGE, cols), 0)
    line = jnp.where(odd_ref[0] == 1, (line + EDGE) % (2 * EDGE), line)
    spot = jnp.where(line < EDGE, line, line + cols - 2 * EDGE)
    spread = jnp.where(lane == spot, 1.0, 0.0)
    odd = odd_ref[1] == 1
    for p, plane_ref in enumerate((source_ref, bed_ref, diff_ref, thick_ref)):
        edges = [even_ref[p], other_ref[p]]
        side = lax.dot_general(
            jnp.concatenate(edges, axis=0),
            spread,
            (((0,), (0,)), ((), ())),
            precision=EXACT,
            preferred_element_type=F32,
        )
        side_ref[p] = side
        first = jnp.concatenate([plane_ref[:EDGE, :], side[:EDGE]], axis=1)
        last = jnp.concatenate(
            [plane_ref[row_count - EDGE :, :], side[row_count - EDGE :]], axis=1
        )
        send_ref[p] = jnp.where(odd, first, last)
        send_other_ref[p] = jnp.where(odd, last, first)


def side(odd, source, bed, diff, thick, edges):
    row_count, cols = source.shape
    strip = jax.ShapeDtypeStruct((4, EDGE, 2 * cols), F32)
    return pl.pallas_call(
        side_kernel,
        in_specs=[SCALARS] + [ON_CHIP] * 6,
        out_specs=[ON_CHIP] * 3,
        out_shape=(jax.ShapeDtypeStruct((4, row_count, cols), F32), strip, strip),
        compiler_params=ROOM,
        cost_estimate=COST,
        name="side",
    )(odd, source, bed, diff, thick, *edges)


def relax_kernel(
    odd_ref, source_ref, bed_ref, diff_ref, start_ref, side_ref, even_ref, other_ref,
    inside_ref, total_ref, mask_ref, thick_ref, field_ref,
):
    row_count, cols = source_ref.shape
    rows, lanes = inside_ref.shape
    ahead = lambda a, axis: pltpu.roll(a, (rows, lanes)[axis] - 1, axis)
    back = lambda a, axis: pltpu.roll(a, 1, axis)
    inside = inside_ref[...]
    odd = odd_ref[1] == 1
    planes = []
    for p, plane_ref in enumerate((source_ref, bed_ref, diff_ref, start_ref)):
        even, other = even_ref[p], other_ref[p]
        planes.append(
            inside
            * jnp.concatenate(
                [
                    jnp.where(odd, even, other),
                    jnp.concatenate([plane_ref[...], side_ref[p]], axis=1),
                    jnp.where(odd, other, even),
                ],
                axis=0,
            )
        )
    source, bed, diff, thick = planes
    source = SMB_RATE * source
    gain = [0.5 * (diff + ahead(diff, axis)) for axis in range(2)]
    for _ in range(STEPS):
        surface = bed + thick
        change = source
        for axis in range(2):
            flow = gain[axis] * (ahead(surface, axis) - surface)
            change = change + (flow - back(flow, axis))
        thick = jnp.maximum(thick + change, 0.0) * inside
    own = thick[EDGE : EDGE + row_count, :cols]
    thick_ref[...] = own
    total = total_ref[...]
    field_ref[0] = ((bed_ref[...] + own) / total).astype(BF16)
    field_ref[1] = (mask_ref[...].astype(F32) * jnp.minimum(own, 1.0) / total).astype(BF16)
    field_ref[2] = (1.0 / total).astype(BF16)


def relax(odd, source, bed, diff, thick, sides, strips, inside, total, mask):
    return pl.pallas_call(
        relax_kernel,
        in_specs=[SCALARS] + [ON_CHIP] * 10,
        out_specs=[ON_CHIP] * 2,
        out_shape=(
            jax.ShapeDtypeStruct(source.shape, F32),
            jax.ShapeDtypeStruct((3,) + source.shape, BF16),
        ),
        compiler_params=ROOM,
        cost_estimate=COST,
        name="relax",
    )(odd, source, bed, diff, thick, sides, *strips, inside, total, mask)


def coupled(
    fluxes, weights, land_rows, owners, elev_class, ice_mask, bed, thickness, diffusivity
):
    groups = lax.axis_size("gx") * lax.axis_size("gy")
    is_ice = lax.axis_index("grp") == 1
    block_weights = weights[0]
    width, row_count, cols = block_weights.shape
    classes, cells = fluxes.shape[1:]
    high_count = cells // LOW

    low_half, high_half, place = head(
        owners.reshape(1, row_count), jnp.transpose(land_rows[0]), groups
    )
    request = jnp.where(is_ice, low_half, swap_cores(high_half))
    asked = lax.all_to_all(request, PLANES, split_axis=0, concat_axis=0, tiled=True)

    flux, bed_now, diff_now, thick_now = lax.optimization_barrier(
        (fluxes[0], bed[0], diffusivity[0], thickness[0], request)
    )[:4]
    table = jnp.pad(flux.astype(BF16), ((0, 16 - classes), (0, 0)))
    table = jnp.transpose(table.reshape(16, high_count, LOW), (1, 0, 2)).reshape(-1, LOW)
    other_table = swap_cores(table)
    table = jnp.where(is_ice, other_table, table)
    at_x, at_y = lax.axis_index("gx"), lax.axis_index("gy")
    odd = jnp.stack([at_y % 2, at_x % 2]).astype(jnp.int32)
    row_at = lax.broadcasted_iota(jnp.int32, (row_count + 2 * EDGE, 2 * cols), 0) - EDGE
    col_at = lax.broadcasted_iota(jnp.int32, (row_count + 2 * EDGE, 2 * cols), 1)
    col_at = jnp.where(col_at < cols + cols // 2, col_at, col_at - 2 * cols)
    inside = (
        ((row_at >= 0) | (at_x > 0))
        & ((row_at < row_count) | (at_x < lax.axis_size("gx") - 1))
        & ((col_at >= 0) | (at_y > 0))
        & ((col_at < cols) | (at_y < lax.axis_size("gy") - 1))
    ).astype(F32)
    line = lax.broadcasted_iota(jnp.int32, (classes * width, 16 * width), 0)
    lane = lax.broadcasted_iota(jnp.int32, (classes * width, 16 * width), 1)
    source_line = ((lane & 127) >> 3) * width + (lane >> 7) * 8 + (lane & 7)
    order = (source_line == line).astype(BF16)

    asked, order, inside, odd = lax.optimization_barrier((asked, order, inside, odd))
    answer = pick(table, asked, classes)
    near = lax.all_to_all(answer, PLANES, split_axis=0, concat_axis=0, tiled=True)
    bed_now, diff_now, thick_now, lower_first = lax.optimization_barrier(
        (bed_now, diff_now, thick_now, odd[0] == 1, answer)
    )[:4]
    turn = lambda cut: jnp.stack([jnp.transpose(a[:, cut]) for a in (bed_now, diff_now, thick_now)])
    first, last = turn(slice(0, EDGE)), turn(slice(cols - EDGE, cols))
    fixed_edges = [jnp.where(lower_first, first, last), jnp.where(lower_first, last, first)]
    near, *fixed_edges = lax.optimization_barrier((near, *fixed_edges))

    near = near.reshape(groups, classes * 128)
    source, total, *edges = remap(
        odd, near, swap_cores(near), place, order, block_weights, elev_class[0], ice_mask[0],
        fixed_edges,
    )
    sides, *strips = side(
        odd, source, bed[0], diffusivity[0], thickness[0], trade_both(*edges, "gy")
    )
    strips = trade_both(*strips, "gx")
    thick, fields = relax(
        odd, source, bed[0], diffusivity[0], thickness[0], sides, strips, inside, total,
        ice_mask[0],
    )

    partial = jnp.einsum("brj,qrj->qrb", block_weights, fields, preferred_element_type=F32)
    outgoing = jnp.einsum(
        "kor,qrb->koqb",
        place.reshape(4, groups, row_count).astype(F32),
        partial,
        precision=EXACT,
        preferred_element_type=F32,
    )
    outgoing = [jnp.concatenate([outgoing[k], outgoing[k + 1]], axis=2) for k in (0, 2)]
    sent = jnp.where(is_ice, outgoing[0], swap_cores(outgoing[1]))
    arrived = lax.all_to_all(
        sent.reshape(groups, -1), PLANES, split_axis=0, concat_axis=0, tiled=True
    )
    land_sums = scatter(asked, arrived.reshape(3 * groups, 128), high_count)
    land_sums = (land_sums + swap_cores(land_sums)).reshape(3, cells)
    averaged = land_sums[:2] / jnp.maximum(land_sums[2], 1.0)
    land_fields = jnp.where(is_ice, 0.0, averaged)[None]
    thickness_new = jnp.where(is_ice, thick, 0.0)[None]
    return (land_fields, thickness_new)


def solution(mesh):
    return jax.shard_map(
        coupled,
        mesh=mesh,
        in_specs=(
            P("grp", None, ("gx", "gy")),
            P("grp", None, "gx", "gy"),
            P("grp", "gx", "gy"),
            P("grp", "gx", "gy", None, None),
            P("grp", "gx", "gy"),
            P("grp", "gx", "gy"),
            P("grp", "gx", "gy"),
            P("grp", "gx", "gy"),
            P("grp", "gx", "gy"),
        ),
        out_specs=(P("grp", None, ("gx", "gy")), P("grp", "gx", "gy")),
        check_vma=False,
    )
```
